32 devices in a mesh: dp: 32 (over z, y, x, core).
Axes of the slice: x: 2, y: 2, z: 4, core: 2. Of those that a mesh axis runs over, the one named last changes fastest.
Arguments:
- tokens: bfloat16 [4096, 1024], P('dp'), may hold values from -6 to 6
- routes: int32 [4096, 8], P('dp'), may hold values from 0 to 31, all different within a row; in each aligned block of 128 rows (0 to 127, 128 to 255, ...) at most 36 rows name the same one
- gain_attn: float32 [1024], replicated, may hold values from 0.25 to 1.75
- w_query: bfloat16 [1024, 1024], replicated, may hold values from -0.1875 to 0.1875
- w_key: bfloat16 [1024, 512], replicated, may hold values from -0.1875 to 0.1875
- w_value: bfloat16 [1024, 512], replicated, may hold values from -0.1875 to 0.1875
- w_out: bfloat16 [1024, 1024], replicated, may hold values from -0.75 to 0.75
- gain_moe: float32 [1024], replicated, may hold values from 0.25 to 1.75
- w_router: bfloat16 [1024, 32], replicated, may hold values from -0.375 to 0.375
- w_gate: bfloat16 [1024, 16384], P(None, 'dp'), may hold values from -0.1875 to 0.1875
- w_up: bfloat16 [1024, 16384], P(None, 'dp'), may hold values from -0.1875 to 0.1875
- w_down: bfloat16 [16384, 1024], P('dp'), may hold values from -0.5 to 0.5
- cotangent: bfloat16 [4096, 1024], P('dp'), may hold values from -6 to 6
Outputs:
- output: bfloat16 [4096, 1024], P('dp')
- d_tokens: bfloat16 [4096, 1024], P('dp')
- grad_gain_attn: float32 [1024], replicated
- grad_w_query: float32 [1024, 1024], replicated
- grad_w_key: float32 [1024, 512], replicated
- grad_w_value: float32 [1024, 512], replicated
- grad_w_out: float32 [1024, 1024], replicated
- grad_gain_moe: float32 [1024], replicated
- grad_w_router: float32 [1024, 32], replicated
- grad_w_gate: float32 [1024, 16384], P(None, 'dp')
- grad_w_up: float32 [1024, 16384], P(None, 'dp')
- grad_w_down: float32 [16384, 1024], P('dp')
The draws below stay inside these ranges and needn't reach their ends.
Inputs may be any that keep to these rules, and one draw needn't show every extreme that they name: `routes`: among the rows of one device no expert is named more than 36 times, a bound that some block reaches; a row names 8 different experts.
All inputs are finite; a program needn't handle non-finite values.
Results may differ from the reference program's by a relative error of at most 0.015.
The reference program's roundings to bfloat16 on the way count: a program that leaves them out, or rounds other values in their place, can miss the bound.
Values may be sent and summed in bfloat16 or wider, within the bound.
No kernel may reach another device: no remote copies, remote signals or barrier semaphores. Data moves between devices by JAX's collectives and lax.ppermute only.
A program may use at most 192 MiB of HBM per device.

```python
import math
import jax
import jax.numpy as jnp
import numpy as np
from jax import lax

D = 1024
HEADS = 16
KV_HEADS = 8
HEAD_DIM = 64
FF = 512
EXPERTS = 32
TOP = 8
TOK_DEV = 128
SHARDS = 1
FF_DEV = 512
TOKENS = 4096
CAP = 36
N_DP = 32


def block_levels(key, dims, cuts, least, high):
    def one(dim, blocks):
        steps = jax.random.uniform(jax.random.fold_in(jax.random.fold_in(key, 6), dim), (blocks,), jnp.float32, least / len(cuts), high / len(cuts))
        return jnp.repeat(jnp.exp(steps), dims[dim] // blocks).reshape((-1,) + (1,) * (len(dims) - dim - 1))

    level = one(*cuts[0])
    for cut in cuts[1:]:
        level = level * one(*cut)
    return level


def shared_out(rng, own, number, rows, count, top, most, skew):
    ranking = jax.random.permutation(rng, count)
    heavy_load, common = load_shares(count, rows * top, most, skew, True), load_shares(count, rows * top, most, skew, False)
    places = jnp.arange(count)

    def named(tallies, rotation):
        used = int((tallies > 0).sum())
        fixed = max(1, used // 4)
        moved = fixed + (places - fixed + rotation * (used - fixed)) % max(1, count - fixed)
        return jnp.zeros((count,), jnp.int32).at[ranking[jnp.where(places < fixed, places, moved)]].set(jnp.asarray(tallies, jnp.int32))

    tallies = jnp.where(number % 4 == 0, named(heavy_load, number // 4), named(common, number - number // 4 - 1))
    mixed = jax.random.permutation(jax.random.fold_in(own, 3), count)
    giver, receiver = mixed[0:count // 2 * 2:2], mixed[1:count // 2 * 2:2]
    room = jnp.minimum(tallies[giver] - 1, most - tallies[receiver]) // 2
    room = jnp.where((giver == ranking[0]) | (receiver == ranking[0]) | (tallies[receiver] == 0), 0, jnp.maximum(room, 0))
    moved = jax.random.randint(jax.random.fold_in(own, 4), (count // 2,), 0, 1 << 20) % (room + 1)
    tallies = tallies.at[giver].add(-moved).at[receiver].add(moved)
    labels = jnp.searchsorted(jnp.cumsum(tallies), jnp.arange(rows * top), side="right").astype(jnp.int32)
    listing = labels.reshape(top, rows).T
    listing = listing[jax.random.permutation(jax.random.fold_in(own, 1), rows)]
    rotation = jax.random.randint(jax.random.fold_in(own, 2), (rows, 1), 0, top)
    return jnp.take_along_axis(listing, (jnp.arange(top)[None, :] + rotation) % top, axis=1)


def load_shares(number_of, total, most, lean, full):
    portions = [(1 << 20) // math.isqrt(grade ** lean) + 1 for grade in range(1, number_of + 1)]
    largest = most if full else min(most, max(-(-total // number_of), total * portions[0] // sum(portions)))
    least = 1 if total - largest >= number_of - 1 else 0
    holding, rest = [largest] + [least] * (number_of - 1), total - largest - least * (number_of - 1)
    while rest > 0:
        free = [i for i in range(1, number_of) if holding[i] < largest] or [i for i in range(1, number_of) if holding[i] < most]
        whole, budget = sum([portions[i] for i in free]), rest
        for i in free:
            more = min(most - holding[i], max(1, budget * portions[i] // whole), rest)
            holding[i] = holding[i] + more
            rest = rest - more
    return np.array(holding)


def noise(own_key, shape, width, limit, cuts=(), held_as=jnp.bfloat16):
    array = width * jax.random.normal(own_key, shape, jnp.float32)
    if cuts:
        array = array * block_levels(own_key, shape, cuts, -0.22, 0.18)
    return jnp.clip(array, -limit, limit).astype(held_as)


def setup_inputs(seed: int = 0) -> dict:
    splits = jax.random.split(jax.random.key(seed), 14)
    tokens = noise(splits[0], (TOKENS, D), 1.0, 6.0, ((0, 32),))
    routes_keys = jax.random.split(jax.random.fold_in(splits[1], 1), TOKENS // TOK_DEV)
    routes_turns = jax.random.permutation(jax.random.fold_in(splits[1], 3), TOKENS // TOK_DEV)
    routes = jax.vmap(lambda own, number: shared_out(jax.random.fold_in(splits[1], 2), own, number, TOK_DEV, EXPERTS, TOP, CAP, 1))(routes_keys, routes_turns).reshape((TOKENS, TOP))
    gain_attn = jnp.clip(1.0 + 0.15 * jax.random.normal(splits[2], (D,), jnp.float32), 0.25, 1.75)
    w_query = noise(splits[3], (D, HEADS * HEAD_DIM), D ** -0.5, 0.1875)
    w_key = noise(splits[4], (D, KV_HEADS * HEAD_DIM), D ** -0.5, 0.1875)
    w_value = noise(splits[5], (D, KV_HEADS * HEAD_DIM), D ** -0.5, 0.1875)
    w_out = noise(splits[6], (HEADS * HEAD_DIM, D), HEAD_DIM ** -0.5, 0.75)
    gain_moe = jnp.clip(1.0 + 0.15 * jax.random.normal(splits[7], (D,), jnp.float32), 0.25, 1.75)
    w_router = noise(splits[8], (D, EXPERTS), (D // 4) ** -0.5, 0.375)
    w_gate = noise(splits[9], (D, EXPERTS * FF), D ** -0.5, 0.1875, ((1, 32),))
    w_up = noise(splits[10], (D, EXPERTS * FF), D ** -0.5, 0.1875, ((1, 32),))
    w_down = noise(splits[11], (EXPERTS * FF, D), (FF // 4) ** -0.5, 0.5, ((0, 32),))
    cotangent = noise(splits[12], (TOKENS, D), 1.0, 6.0, ((0, 32),))
    return dict(tokens=tokens, routes=routes, gain_attn=gain_attn, w_query=w_query, w_key=w_key, w_value=w_value, w_out=w_out, gain_moe=gain_moe, w_router=w_router, w_gate=w_gate, w_up=w_up, w_down=w_down, cotangent=cotangent)


epsilon = 1e-06
highest = lax.Precision.HIGHEST

@jax.custom_vjp
def low(v):
    return lax.optimization_barrier(v.astype(jnp.bfloat16)).astype(jnp.float32)

@jax.custom_vjp
def low_back(v):
    return v

def low_keep(v):
    return (low(v), None)

def low_pass(kept, grad):
    return (grad,)

def back_keep(v):
    return (v, None)

def back_low(kept, grad):
    return (low(grad),)
low.defvjp(low_keep, low_pass)
low_back.defvjp(back_keep, back_low)

def matmul_high(left, right):
    return jnp.dot(left, right, precision=highest, preferred_element_type=jnp.float32)

def normalize(values, gain):
    factor = lax.rsqrt(lax.optimization_barrier(jnp.mean(values * values, axis=-1, keepdims=True)) + epsilon)
    return values * factor * gain

def rope_tables(length):
    half = HEAD_DIM // 2
    positions = jnp.arange(length, dtype=jnp.float32)[:, None]
    frequency = jnp.exp(jnp.arange(half, dtype=jnp.float32) * (-2.0 * math.log(10000.0) / HEAD_DIM))
    angles = positions * frequency[None, :]
    return (jnp.cos(angles), jnp.sin(angles))

def rotate(values, cosine, sine):
    half = values.shape[-1] // 2
    first = values[..., :half]
    second = values[..., half:]
    return jnp.concatenate([first * cosine - second * sine, second * cosine + first * sine], axis=-1)

def attend(normed, w_query, w_key, w_value):
    length = normed.shape[0]
    group = HEADS // KV_HEADS
    cosine, sine = rope_tables(length)
    query_pre = low_back(matmul_high(normed, w_query)).reshape(length, KV_HEADS, group, HEAD_DIM)
    queries = low(rotate(query_pre, cosine[:, None, None, :], sine[:, None, None, :]))
    key_pre = low_back(matmul_high(normed, w_key)).reshape(length, KV_HEADS, HEAD_DIM)
    keys = low(rotate(key_pre, cosine[:, None, :], sine[:, None, :]))
    values = low(low_back(matmul_high(normed, w_value))).reshape(length, KV_HEADS, HEAD_DIM)
    scores = jnp.einsum('qkgd,jkd->kgqj', queries, keys, precision=highest) * 0.125
    causal = jnp.arange(length)[:, None] >= jnp.arange(length)[None, :]
    scores = low_back(jnp.where(causal, scores, -1e+30))
    weights = jax.nn.softmax(scores, axis=-1)
    mixed = jnp.einsum('kgqj,jkd->qkgd', low(weights), values, precision=highest)
    return mixed.reshape(length, HEADS * HEAD_DIM)

def reference(tokens, routes, gain_attn, w_query, w_key, w_value, w_out, gain_moe, w_router, w_gate, w_up, w_down, cotangent):
    per_device = TOK_DEV * TOP
    flat_routes = routes.reshape(N_DP, per_device)
    marks = (flat_routes[:, :, None] == jnp.arange(EXPERTS, dtype=jnp.int32)[None, None, :]).astype(jnp.int32)
    ranks = lax.optimization_barrier(jnp.sum((jnp.cumsum(marks, axis=1) - 1) * marks, axis=-1)).astype(jnp.int32)
    position = jnp.arange(N_DP, dtype=jnp.int32)[:, None] * CAP + ranks
    assignment = jnp.arange(TOKENS * TOP, dtype=jnp.int32).reshape(N_DP, per_device)
    table = jnp.full((EXPERTS, N_DP * CAP), TOKENS * TOP, jnp.int32).at[flat_routes, position].set(assignment)
    picks = routes[:, :, None] == jnp.arange(EXPERTS, dtype=jnp.int32)[None, None, :]

    def forward(inputs, gain_one, query_w, key_w, value_w, out_w, gain_two, router_w, gate_w, up_w, down_w):
        normed1 = low(normalize(inputs, gain_one))

        def one_sequence(normed):
            return attend(normed, query_w, key_w, value_w)
        attended = lax.map(jax.checkpoint(one_sequence), normed1.reshape(N_DP, TOK_DEV, D))
        attended = low_back(low(attended.reshape(TOKENS, HEADS * HEAD_DIM)))
        hidden1 = inputs + low_back(matmul_high(attended, out_w))
        normed2 = low(normalize(hidden1, gain_two))
        logits = low_back(matmul_high(normed2, router_w))
        chosen = lax.optimization_barrier(jnp.sum(jnp.where(picks, logits[:, None, :], 0.0), axis=-1))
        gates = jax.nn.softmax(chosen, axis=-1)
        gate_flat = jnp.concatenate([gates.reshape(-1), jnp.zeros((1,), jnp.float32)])
        padded = jnp.concatenate([normed2, jnp.zeros((1, D), jnp.float32)], axis=0)
        gate_stack = gate_w.reshape(D, EXPERTS, FF).transpose(1, 0, 2)
        up_stack = up_w.reshape(D, EXPERTS, FF).transpose(1, 0, 2)
        down_stack = down_w.reshape(EXPERTS, FF, D)

        def expert_step(total, pieces):
            slots, gate_weight, up_weight, down_weight = pieces
            token_index = slots // TOP
            produced = jnp.zeros((slots.shape[0], D), jnp.float32)
            for block_index in range(SHARDS):
                first = block_index * FF_DEV
                rows = low_back(padded[token_index])
                gate_pre = low_back(matmul_high(rows, gate_weight[:, first:first + FF_DEV]))
                up_pre = low_back(matmul_high(rows, up_weight[:, first:first + FF_DEV]))
                activated = low(jax.nn.silu(gate_pre) * up_pre)
                produced = produced + low(low_back(matmul_high(activated, down_weight[first:first + FF_DEV])))
            total = total.at[token_index].add(gate_flat[slots][:, None] * produced)
            return (total, None)
        start_total = jnp.zeros((TOKENS + 1, D), jnp.float32)
        total, unused = lax.scan(jax.checkpoint(expert_step), start_total, (table, gate_stack, up_stack, down_stack))
        return hidden1 + total[:TOKENS]
    primals = (tokens.astype(jnp.float32), gain_attn, w_query.astype(jnp.float32), w_key.astype(jnp.float32), w_value.astype(jnp.float32), w_out.astype(jnp.float32), gain_moe, w_router.astype(jnp.float32), w_gate.astype(jnp.float32), w_up.astype(jnp.float32), w_down.astype(jnp.float32))
    result, pullback = jax.vjp(forward, *primals)
    grads = pullback(cotangent.astype(jnp.float32))
    return (result.astype(jnp.bfloat16), grads[0].astype(jnp.bfloat16), grads[1], grads[2], grads[3], grads[4], grads[5], grads[6], grads[7], grads[8], grads[9], grads[10])
```

```python
import functools
import math

import jax
import jax.numpy as jnp
import numpy as np
from jax import lax
from jax.experimental import pallas as pl
from jax.experimental.pallas import tpu as pltpu
from jax.sharding import PartitionSpec as P

D = 1024
HEADS = 16
KV_HEADS = 8
HEAD_DIM = 64
EXPERTS = 32
TOP = 8
TOK = 128
ZN = 4
EP = EXPERTS // ZN
CAPZ = 144
EXTRA = CAPZ + 8
EPS = 1e-06

f32 = jnp.float32
bf16 = jnp.bfloat16


def rope_constants():
    half = HEAD_DIM // 2
    angles = np.arange(TOK)[:, None] * np.exp(
        np.arange(half) * (-2.0 * math.log(10000.0) / HEAD_DIM)
    )[None, :]
    lanes = np.arange(128) % half
    return (
        np.cos(angles)[:, lanes].astype(np.float32),
        np.sin(angles)[:, lanes].astype(np.float32),
    )


def iota(shape, dim):
    return lax.broadcasted_iota(jnp.int32, shape, dim)


def dot(a, b, ca=1, cb=0):
    return lax.dot_general(a, b, (((ca,), (cb,)), ((), ())), preferred_element_type=f32)


def split2(v):
    hi = v.astype(bf16)
    return hi, (v - hi.astype(f32)).astype(bf16)


def split3(v):
    hi, rest = v.astype(bf16), v - v.astype(bf16).astype(f32)
    mid, low = split2(rest)
    return hi, mid, low


def rotate_slab(x, cosine, sine):
    low_half = (iota(x.shape, 1) % HEAD_DIM) < HEAD_DIM // 2
    ahead = pltpu.roll(x, 128 - HEAD_DIM // 2, 1)
    behind = pltpu.roll(x, HEAD_DIM // 2, 1)
    return x * cosine + jnp.where(low_half, -ahead, behind) * sine


def norm_parts(x):
    scale = lax.rsqrt(jnp.mean(x * x, axis=-1, keepdims=True) + EPS)
    return scale, x * scale


def mask_rows(routes_t, q):
    expert = iota((EP, TOK), 0) + EP * q
    hit = routes_t[0:1, :] == expert
    for k in range(1, TOP):
        hit = hit | (routes_t[k : k + 1, :] == expert)
    return hit


def causal_mask():
    return iota((TOK, 2 * TOK), 0) >= (iota((TOK, 2 * TOK), 1) % TOK)


def stack_halves(slab):
    left = (iota((TOK, 128), 1) < HEAD_DIM).astype(f32).astype(bf16)
    right = (iota((TOK, 128), 1) >= HEAD_DIM).astype(f32).astype(bf16)
    return jnp.concatenate([slab * left, slab * right], axis=0)


def softmax_pair(scores):
    parts = []
    for i in range(2):
        s = scores[:, 128 * i : 128 * i + 128]
        e = jnp.exp(s - jnp.max(s, axis=-1, keepdims=True))
        parts.append(e / jnp.sum(e, axis=-1, keepdims=True))
    return parts


def pair_scores(q_slab, k_stack, causal):
    return jnp.where(causal, dot(q_slab, k_stack, 1, 1) * 0.125, -1e30)


def lanes(x, i):
    return x[:, 128 * i : 128 * i + 128]


def call(body, name, ins, outs, scratch=(), grid=None, in_specs=None, out_specs=None, flops=0, nbytes=0):
    vm = pl.BlockSpec(memory_space=pltpu.VMEM)
    return pl.pallas_call(
        body,
        name=name,
        out_shape=outs,
        grid=grid or (),
        in_specs=in_specs or [vm] * len(ins),
        out_specs=out_specs or jax.tree.map(lambda _: vm, outs),
        scratch_shapes=list(scratch),
        compiler_params=pltpu.CompilerParams(vmem_limit_bytes=60 * 1024 * 1024),
        cost_estimate=pl.CostEstimate(flops=flops, bytes_accessed=nbytes, transcendentals=0),
    )(*ins)


def shape(dims, dtype):
    return jax.ShapeDtypeStruct(dims, dtype)


SMEM = pl.BlockSpec(memory_space=pltpu.SMEM)
VM = pl.BlockSpec(memory_space=pltpu.VMEM)
ANY = pl.BlockSpec(memory_space=pl.ANY)


def pack_cotangent(routes_t_ref, cot_ref, out_ref):
    out_ref[0:TOK, :] = cot_ref[...]
    out_ref[TOK:, :] = jnp.zeros((8, D), bf16)
    for q in range(ZN):
        mask = mask_rows(routes_t_ref[...], q)
        out_ref[TOK : TOK + 8, 128 * q : 128 * q + 128] = jnp.where(mask, 1.0, 0.0).astype(bf16)


def attention_forward(
    routes_t_ref, tokens_ref, gain_a_ref, gain_m_ref, cos_ref, sin_ref, wr_ref,
    wq_hbm, wk_hbm, wv_hbm, wo_hbm,
    hidden_ref, pay_ref, q_ref, kd_ref, vd_ref, att_ref, gate_ref,
    wq_ref, wk_ref, wv_ref, wo_ref, sems,
):
    copies = [
        pltpu.make_async_copy(src, dst, sems.at[i])
        for i, (src, dst) in enumerate(
            ((wq_hbm, wq_ref), (wk_hbm, wk_ref), (wv_hbm, wv_ref), (wo_hbm, wo_ref))
        )
    ]
    for copy in copies:
        copy.start()
    x = tokens_ref[...].astype(f32)
    _, plain1 = norm_parts(x)
    normed1 = (plain1 * gain_a_ref[...]).astype(bf16)
    cosine, sine = cos_ref[...], sin_ref[...]
    copies[0].wait()
    query_pre = dot(normed1, wq_ref[...])
    copies[1].wait()
    key_pre = dot(normed1, wk_ref[...])
    copies[2].wait()
    values = dot(normed1, wv_ref[...]).astype(bf16).astype(f32)
    causal = causal_mask()
    first = iota((TOK, 128), 1) < HEAD_DIM
    for pair in range(KV_HEADS // 2):
        k_slab = rotate_slab(lanes(key_pre, pair), cosine, sine)
        v_slab = lanes(values, pair)
        k_roll = pltpu.roll(k_slab, HEAD_DIM, 1)
        v_roll = pltpu.roll(v_slab, HEAD_DIM, 1)
        for side in range(2):
            g = 2 * pair + side
            keep = first if side == 0 else ~first
            k_dup = jnp.where(keep, k_slab, k_roll).astype(bf16)
            v_dup = jnp.where(keep, v_slab, v_roll).astype(bf16)
            q_slab = rotate_slab(lanes(query_pre, g), cosine, sine).astype(bf16)
            span = slice(128 * g, 128 * g + 128)
            q_ref[:, span] = q_slab
            kd_ref[:, span] = k_dup
            vd_ref[:, span] = v_dup
            w0, w1 = softmax_pair(pair_scores(q_slab, stack_halves(k_dup), causal))
            low = jnp.concatenate([w0.astype(bf16), w1.astype(bf16)], axis=1)
            att_ref[:, span] = dot(low, stack_halves(v_dup)).astype(bf16)
    copies[3].wait()
    hidden1 = x + dot(att_ref[...], wo_ref[...])
    hidden_ref[...] = hidden1
    _, plain2 = norm_parts(hidden1)
    normed2 = (plain2 * gain_m_ref[...]).astype(bf16)
    pay_ref[0:TOK, :] = normed2
    logits_t = jnp.transpose(dot(normed2, wr_ref[...]))
    mask = jnp.concatenate([mask_rows(routes_t_ref[...], q) for q in range(ZN)], axis=0)
    chosen = jnp.where(mask, logits_t, -1e30)
    expo = jnp.where(mask, jnp.exp(chosen - jnp.max(chosen, axis=0, keepdims=True)), 0.0)
    gates = expo / jnp.sum(expo, axis=0, keepdims=True)
    gate_ref[...] = gates
    pay_ref[TOK:, :] = jnp.zeros((16, D), bf16)
    for q in range(ZN):
        hi, mid = split2(gates[EP * q : EP * q + EP])
        pay_ref[TOK : TOK + 8, 128 * q : 128 * q + 128] = hi
        pay_ref[TOK + 8 : TOK + 16, 128 * q : 128 * q + 128] = mid


def pick_rows(rank_row):
    slot = iota((CAPZ, rank_row.shape[1]), 0).astype(f32)
    return jnp.where(slot == rank_row, 1.0, 0.0)


def plane_lanes(z):
    return pl.ds(pl.multiple_of(z * 128, 128), 128)


def select_cotangent(z_ref, x0, x1, x2, x3, out_ref, rank_ref, xs):
    half = EP // 2
    step = pl.program_id(0)

    @pl.when(step == 0)
    def _():
        masks = []
        for m, x in enumerate((x0, x1, x2, x3)):
            xs[TOK * m : TOK * m + TOK, :] = x[0:TOK, :]
            masks.append(x[TOK : TOK + 8, plane_lanes(z_ref[0])])
        mask = jnp.concatenate(masks, axis=1)
        width = ZN * TOK
        before = jnp.where(iota((width, width), 0) < iota((width, width), 1), 1.0, 0.0).astype(bf16)
        rank_ref[...] = jnp.where(mask.astype(f32) > 0.5, dot(mask, before), -1.0)

    picks = jnp.concatenate(
        [pick_rows(rank_ref[pl.ds(half * step + i, 1), :]).astype(bf16) for i in range(half)], axis=0
    )
    out_ref[...] = dot(picks, xs[...]).astype(bf16).reshape(half, CAPZ, D)


def select_rows(z_ref, rank_ref, x0, x1, x2, x3, out_ref, gate_ref, xs):
    half = EP // 2
    step = pl.program_id(0)
    his, mids = [], []
    for x in (x0, x1, x2, x3):
        his.append(x[TOK : TOK + 8, plane_lanes(z_ref[0])])
        mids.append(x[TOK + 8 : TOK + 16, plane_lanes(z_ref[0])])
    hi, mid = jnp.concatenate(his, axis=1), jnp.concatenate(mids, axis=1)

    @pl.when(step == 0)
    def _():
        for m, x in enumerate((x0, x1, x2, x3)):
            xs[TOK * m : TOK * m + TOK, :] = x[0:TOK, :]
        gate_ref[...] = hi.astype(f32) + mid.astype(f32)

    picks = [
        pick_rows(rank_ref[pl.ds(half * step + i, 1), :]).astype(bf16) for i in range(half)
    ]
    rows = dot(jnp.concatenate(picks, axis=0), xs[...]).astype(bf16).reshape(half, CAPZ, D)
    out_ref[:, 0:CAPZ, :] = rows
    row = iota((8, CAPZ), 0)
    for i in range(half):
        mine = row == half * step + i
        top = jnp.sum(jnp.where(mine, dot(hi, picks[i], 1, 1), 0.0), axis=0, keepdims=True)
        rest = jnp.sum(jnp.where(mine, dot(mid, picks[i], 1, 1), 0.0), axis=0, keepdims=True)
        out_ref[i, CAPZ:EXTRA, :] = jnp.zeros((8, D), bf16)
        both = jnp.where(row == 0, top, jnp.where(row == 1, rest, 0.0))
        out_ref[i, CAPZ:EXTRA, 0:CAPZ] = both.astype(bf16)


def row_to_column(row):
    return jnp.transpose(jnp.broadcast_to(row, (128, row.shape[1])))[:, 0:1]


def column_to_rows(col):
    pad = jnp.concatenate([col, jnp.zeros((256 - CAPZ, 1), f32)], axis=0)
    return jnp.transpose(jnp.broadcast_to(pad, (256, 128)))[0:8, 0:CAPZ]


def expert_rows(
    x_ref, y_ref, wg_ref, wu_ref, wd_ref,
    prod_ref, back_ref, act_ref, dprod_ref, dgate_ref, dup_ref,
):
    part = x_ref.shape[0]
    rows = part * CAPZ
    x = x_ref[:, 0:CAPZ, :].reshape(rows, D)
    upstream = y_ref[...].reshape(rows, D).astype(f32)
    columns = []
    for b in range(part):
        extra = x_ref[b, CAPZ:EXTRA, 0:256].astype(f32)
        columns.append(row_to_column(extra[0:1] + extra[1:2])[0:CAPZ])
    gate_col = jnp.concatenate(columns, axis=0)
    gate_pre = dot(x, wg_ref[...])
    up_pre = dot(x, wu_ref[...])
    sig = jax.nn.sigmoid(gate_pre)
    silu = gate_pre * sig
    act = (silu * up_pre).astype(bf16)
    act_ref[...] = act
    produced = dot(act, wd_ref[...]).astype(bf16)
    prod_ref[...] = produced.reshape(part, CAPZ, D)
    d_gates = jnp.sum(upstream * produced.astype(f32), axis=-1, keepdims=True)
    d_prod = (gate_col * upstream).astype(bf16)
    dprod_ref[...] = d_prod
    d_act = dot(d_prod, wd_ref[...], 1, 1)
    d_gate = (d_act * up_pre * sig * (1.0 + gate_pre * (1.0 - sig))).astype(bf16)
    d_up = (d_act * silu).astype(bf16)
    dgate_ref[...] = d_gate
    dup_ref[...] = d_up
    d_rows = dot(d_gate, wg_ref[...], 1, 1) + dot(d_up, wu_ref[...], 1, 1)
    back_ref[:, 0:CAPZ, :] = d_rows.astype(bf16).reshape(part, CAPZ, D)
    row = iota((8, CAPZ), 0)
    for b in range(part):
        hi, mid, low = split3(column_to_rows(d_gates[CAPZ * b : CAPZ * b + CAPZ]))
        hi, mid, low = hi.astype(f32), mid.astype(f32), low.astype(f32)
        out = jnp.where(row == 0, hi, jnp.where(row == 1, mid, jnp.where(row == 2, low, 0.0)))
        back_ref[b, CAPZ:EXTRA, :] = jnp.zeros((8, D), bf16)
        back_ref[b, CAPZ:EXTRA, 0:CAPZ] = out.astype(bf16)


def expert_weights(x_ref, act_ref, dprod_ref, dgate_ref, dup_ref, gg_ref, gu_ref, gd_ref):
    part = x_ref.shape[0]
    x = x_ref[:, 0:CAPZ, :].reshape(part * CAPZ, D)

    @pl.when(pl.program_id(0) == 0)
    def _():
        gg_ref[...] = jnp.zeros_like(gg_ref)
        gu_ref[...] = jnp.zeros_like(gu_ref)
        gd_ref[...] = jnp.zeros_like(gd_ref)

    gg_ref[...] += dot(x, dgate_ref[...], 0, 0)
    gu_ref[...] += dot(x, dup_ref[...], 0, 0)
    gd_ref[...] += dot(act_ref[...], dprod_ref[...], 0, 0)


def combine_back(shards, back_ref, rank_ref, out_ref, acc, dg):
    step = pl.program_id(0)
    part = back_ref.shape[0]

    @pl.when(step == 0)
    def _():
        dg[...] = jnp.zeros_like(dg)

    picks = []
    row8 = iota((8, ZN * TOK), 0)
    for i in range(part):
        e = (part * step + i) // shards
        pick = pick_rows(rank_ref[pl.ds(e, 1), :]).astype(bf16)
        picks.append(pick)
        sums = dot(back_ref[i, CAPZ:EXTRA, 0:CAPZ], pick)
        dg[...] += jnp.where(row8 == e, jnp.sum(sums[0:3], axis=0, keepdims=True), 0.0)
    rows = back_ref[:, 0:CAPZ, :].reshape(part * CAPZ, D)
    total = dot(jnp.concatenate(picks, axis=0), rows, 0, 0)

    @pl.when(step == 0)
    def _():
        acc[...] = total

    @pl.when(step > 0)
    def _():
        acc[...] += total

    @pl.when(step == pl.num_programs(0) - 1)
    def _():
        for m in range(ZN):
            out_ref[m, 0:TOK, :] = acc[TOK * m : TOK * m + TOK, :].astype(bf16)
            out_ref[m, TOK:, :] = jnp.zeros((24, D), bf16)
            parts = split3(dg[:, TOK * m : TOK * m + TOK])
            for i, piece in enumerate(parts):
                out_ref[m, TOK + 8 * i : TOK + 8 * i + 8, 0:TOK] = piece


def combine_output(shards, back_ref, rank_ref, gate_ref, out_ref, acc):
    step = pl.program_id(0)
    part = back_ref.shape[0]
    picks, scaled = [], []
    for i in range(part):
        e = (part * step + i) // shards
        pick = pick_rows(rank_ref[pl.ds(e, 1), :])
        picks.append(pick.astype(bf16))
        col = jnp.sum(pick * gate_ref[pl.ds(e, 1), :], axis=-1, keepdims=True)
        scaled.append((back_ref[i].astype(f32) * col).astype(bf16))
    total = dot(jnp.concatenate(picks, axis=0), jnp.concatenate(scaled, axis=0), 0, 0)

    @pl.when(step == 0)
    def _():
        acc[...] = total

    @pl.when(step > 0)
    def _():
        acc[...] += total

    @pl.when(step == pl.num_programs(0) - 1)
    def _():
        for m in range(ZN):
            out_ref[m] = acc[TOK * m : TOK * m + TOK, :].astype(bf16)


def final_output(hidden_ref, p0, p1, p2, p3, out_ref):
    total = (p0[...].astype(f32) + p1[...].astype(f32)) + (p2[...].astype(f32) + p3[...].astype(f32))
    out_ref[...] = (hidden_ref[...] + total).astype(bf16)


def extra_rows(block):
    return -(-block // 16) * 16


def store_blocks(out_ref, me, value, base, block):
    for i in range(value.shape[0] // block):
        out_ref[(base + i) ^ me, 0:block, :] = value[block * i : block * i + block]


def hidden_backward(
    scal_ref, p0, p1, p2, p3, hidden_ref, cot_ref, gate_ref, pay_ref, att_ref, wr_ref, gain_m_ref,
    wo_ref, dh_ref, datt_ref, go_ref,
):
    z, me = scal_ref[0], scal_ref[1]
    n, block = go_ref.shape[0], D // go_ref.shape[0]
    pieces = (p0, p1, p2, p3)
    dgs = []
    for p in pieces:
        e = p[TOK:, 0:TOK].astype(f32)
        dgs.append(e[0:8] + e[8:16] + e[16:24])
    blocks = []
    for q in range(ZN):
        total = jnp.zeros((8, TOK), f32)
        for m in range(ZN):
            total += jnp.where((z ^ m) == q, dgs[m], 0.0)
        blocks.append(total)
    d_gates = jnp.concatenate(blocks, axis=0)
    gates = gate_ref[...]
    d_chosen = gates * (d_gates - jnp.sum(gates * d_gates, axis=0, keepdims=True))
    d_logits_t = d_chosen.astype(bf16)
    pad = jnp.concatenate([d_chosen, jnp.zeros((TOK - EXPERTS, TOK), f32)], axis=0)
    d_logits = jnp.transpose(pad)[:, 0:EXPERTS].astype(bf16)
    rows = [p[0:TOK, :].astype(f32) for p in pieces]
    d_normed2 = (rows[0] + rows[1]) + (rows[2] + rows[3]) + dot(d_logits, wr_ref[...], 1, 1)
    router = dot(d_logits_t, pay_ref[0:TOK, :])
    scale2, plain2 = norm_parts(hidden_ref[...])
    gain = jnp.sum(d_normed2 * plain2, axis=0, keepdims=True)
    u = d_normed2 * gain_m_ref[...]
    d_hidden = cot_ref[...].astype(f32) + scale2 * (
        u - plain2 * jnp.mean(u * plain2, axis=-1, keepdims=True)
    )
    dh_ref[...] = d_hidden
    d_attn = d_hidden.astype(bf16)
    datt_ref[...] = dot(d_attn, wo_ref[...], 1, 1).astype(bf16)
    for c in range(4):
        piece = dot(att_ref[:, 256 * c : 256 * c + 256], d_attn, 0, 0).astype(bf16)
        store_blocks(go_ref, me, piece, 256 * c // block, block)
    row = iota((8, D), 0)
    first = extra_rows(block)
    step = n // EXPERTS
    for i in range(n):
        value = jnp.zeros((8, D), f32)
        if i % step == 0:
            value = jnp.where(row == 0, router[i // step : i // step + 1, :], value)
        if i == 0:
            value = jnp.where(row == 1, gain, value)
        if first > block:
            go_ref[i ^ me, block:first, :] = jnp.zeros((first - block, D), bf16)
        go_ref[i ^ me, first : first + 8, :] = value.astype(bf16)


def attention_backward(
    scal_ref, tokens_ref, gain_a_ref, cos_ref, sin_ref, q_ref, kd_ref, vd_ref, datt_ref, dh_ref,
    wq_hbm, wk_hbm, wv_hbm,
    dtok_ref, gq_ref, gkv_ref,
    wq_ref, wk_ref, wv_ref, dq_ref, dk_ref, dv_ref, sems,
):
    me_q, me_kv = scal_ref[2], scal_ref[3]
    n, block = gq_ref.shape[0], D // gq_ref.shape[0]
    copies = [
        pltpu.make_async_copy(src, dst, sems.at[i])
        for i, (src, dst) in enumerate(((wq_hbm, wq_ref), (wk_hbm, wk_ref), (wv_hbm, wv_ref)))
    ]
    for copy in copies:
        copy.start()
    x = tokens_ref[...].astype(f32)
    scale1, plain1 = norm_parts(x)
    normed1 = (plain1 * gain_a_ref[...]).astype(bf16)
    cosine, sine = cos_ref[...], -sin_ref[...]
    causal = causal_mask()
    first = iota((TOK, 128), 1) < HEAD_DIM
    for pair in range(KV_HEADS // 2):
        dks, dvs = [], []
        for side in range(2):
            g = 2 * pair + side
            span = slice(128 * g, 128 * g + 128)
            q_slab, da_slab = q_ref[:, span], datt_ref[:, span]
            k_stack = stack_halves(kd_ref[:, span])
            weights = softmax_pair(pair_scores(q_slab, k_stack, causal))
            d_weights = dot(da_slab, stack_halves(vd_ref[:, span]), 1, 1)
            lows, d_lows = [], []
            for i in range(2):
                w, dw = weights[i], lanes(d_weights, i)
                lows.append(w.astype(bf16))
                d_lows.append((w * (dw - jnp.sum(w * dw, axis=-1, keepdims=True))).astype(bf16))
            d_scores = jnp.concatenate(d_lows, axis=1)
            low = jnp.concatenate(lows, axis=1)
            d_q = dot(d_scores, k_stack) * 0.125
            dq_ref[:, span] = rotate_slab(d_q, cosine, sine).astype(bf16)
            d_k2 = dot(d_scores, q_slab, 0, 0) * 0.125
            d_v2 = dot(low, da_slab, 0, 0)
            d_k = jnp.where(first, d_k2[0:TOK], d_k2[TOK:])
            d_v = jnp.where(first, d_v2[0:TOK], d_v2[TOK:])
            d_k = d_k + pltpu.roll(d_k, HEAD_DIM, 1)
            d_v = d_v + pltpu.roll(d_v, HEAD_DIM, 1)
            dks.append(rotate_slab(d_k, cosine, sine))
            dvs.append(d_v)
        span = slice(128 * pair, 128 * pair + 128)
        dk_ref[:, span] = jnp.where(first, dks[0], dks[1]).astype(bf16)
        dv_ref[:, span] = jnp.where(first, dvs[0], dvs[1]).astype(bf16)
    d_q, d_k, d_v = dq_ref[...], dk_ref[...], dv_ref[...]
    for copy in copies:
        copy.wait()
    d_normed1 = dot(d_q, wq_ref[...], 1, 1) + dot(d_k, wk_ref[...], 1, 1) + dot(d_v, wv_ref[...], 1, 1)
    gain = jnp.sum(d_normed1 * plain1, axis=0, keepdims=True)
    u = d_normed1 * gain_a_ref[...]
    d_tokens = dh_ref[...] + scale1 * (u - plain1 * jnp.mean(u * plain1, axis=-1, keepdims=True))
    dtok_ref[...] = d_tokens.astype(bf16)
    d_kv = jnp.concatenate([d_k, d_v], axis=1)
    for c in range(4):
        left = normed1[:, 256 * c : 256 * c + 256]
        store_blocks(gq_ref, me_q, dot(left, d_q, 0, 0).astype(bf16), 256 * c // block, block)
        store_blocks(gkv_ref, me_kv, dot(left, d_kv, 0, 0).astype(bf16), 256 * c // block, block)
    start = extra_rows(block)
    row = iota((8, D), 0)
    for i in range(n):
        value = jnp.where(row == 1, gain, 0.0) if i == 0 else jnp.zeros((8, D), f32)
        if start > block:
            gkv_ref[i ^ me_kv, block:start, :] = jnp.zeros((start - block, D), bf16)
        gkv_ref[i ^ me_kv, start : start + 8, :] = value.astype(bf16)


def swap(x, n, mask):
    return lax.ppermute(x, "dp", [(i, i ^ mask) for i in range(n)])


def owner_code(me, order):
    code = 0
    for bit in order:
        code = code * 2 + (me // (1 << bit)) % 2
    return code


def scatter_sum(x, n, order):
    for bit in order[:-2]:
        half = x.shape[0] // 2
        got = swap(x[half:], n, 1 << bit)
        x = (x[:half].astype(f32) + got.astype(f32)).astype(bf16)
    g = n // ZN
    got = [swap(x[m], n, m * g) for m in range(1, ZN)]
    parts = [x[0].astype(f32)] + [v.astype(f32) for v in got]
    return ((parts[0] + parts[1]) + (parts[2] + parts[3])).astype(bf16)[None]


def gather_back(x, n, order):
    g = n // ZN
    x = jnp.concatenate([x] + [swap(x, n, m * g) for m in range(1, ZN)], axis=0)
    for bit in reversed(order[:-2]):
        x = jnp.concatenate([x, swap(x, n, 1 << bit)], axis=0)
    return x


def finish_grad(me, x_ref, out_ref):
    n, block = x_ref.shape[0], D // x_ref.shape[0]
    for i in range(n):
        out_ref[block * i : block * i + block, :] = x_ref[i ^ me, 0:block, :].astype(f32)


def finish_plain(slot, scal_ref, x_ref, out_ref):
    finish_grad(scal_ref[slot], x_ref, out_ref)


def finish_extra(slot, rows, scal_ref, x_ref, out_ref, extra_ref):
    me = scal_ref[slot]
    finish_grad(me, x_ref, out_ref)
    n, start = x_ref.shape[0], extra_rows(D // x_ref.shape[0])
    step = n // EXPERTS
    for i in range(EXPERTS):
        extra_ref[8 * i : 8 * i + 8, :] = x_ref[(i * step) ^ me, start : start + 8, :].astype(f32)


def finish_kv(slot, scal_ref, x_ref, k_ref, v_ref, extra_ref):
    me = scal_ref[slot]
    n, block = x_ref.shape[0], D // x_ref.shape[0]
    for i in range(n):
        value = x_ref[i ^ me, 0:block, :].astype(f32)
        k_ref[block * i : block * i + block, :] = value[:, 0 : D // 2]
        v_ref[block * i : block * i + block, :] = value[:, D // 2 :]
    start = extra_rows(block)
    extra_ref[...] = x_ref[me, start : start + 8, :].astype(f32)


def body(
    tokens, routes, gain_attn, w_query, w_key, w_value, w_out, gain_moe, w_router,
    w_gate, w_up, w_down, cotangent,
):
    n = lax.axis_size("dp")
    plane = n // ZN
    shards = n // EXPERTS
    hidden_units = w_gate.shape[1]
    groups = [[z * plane + j for j in range(plane)] for z in range(ZN)]
    bits = int(math.log2(n))
    inner = list(range(1, bits - 2))
    cut = len(inner) // 2
    top = [bits - 1, bits - 2]
    order_q = [0] + inner + top
    order_kv = [0] + inner[cut:] + inner[:cut] + top
    order_o = order_q
    me = lax.axis_index("dp").astype(jnp.int32)
    z = me // plane
    scal = jnp.stack(
        [z, owner_code(me, order_o), owner_code(me, order_q), owner_code(me, order_kv)]
    ).astype(jnp.int32)
    cos_np, sin_np = rope_constants()
    cosine, sine = jnp.asarray(cos_np), jnp.asarray(sin_np)
    gain_a, gain_m = gain_attn.reshape(1, D), gain_moe.reshape(1, D)
    routes_t = routes.T

    def exchange(x):
        return [x] + [swap(x, n, m * plane) for m in range(1, ZN)]

    def plane_exchange(x):
        return lax.all_to_all(x, "dp", 0, 0, tiled=True, axis_index_groups=groups)

    def spread(x):
        return x if shards == 1 else jnp.repeat(x, shards, axis=0)

    pay3 = call(
        pack_cotangent, "pack_cotangent", (routes_t, cotangent), shape((TOK + 8, D), bf16),
        flops=0, nbytes=600_000,
    )
    cots = exchange(pay3)
    hidden1, pay1, q, kd, vd, attended, gates = call(
        attention_forward, "attention_forward",
        (routes_t, tokens, gain_a, gain_m, cosine, sine, w_router, w_query, w_key, w_value, w_out),
        (
            shape((TOK, D), f32), shape((TOK + 16, D), bf16), shape((TOK, D), bf16),
            shape((TOK, D), bf16), shape((TOK, D), bf16), shape((TOK, D), bf16),
            shape((EXPERTS, TOK), f32),
        ),
        in_specs=[VM] * 7 + [ANY] * 4,
        scratch=(
            pltpu.VMEM((D, D), bf16), pltpu.VMEM((D, D // 2), bf16), pltpu.VMEM((D, D // 2), bf16),
            pltpu.VMEM((D, D), bf16), pltpu.SemaphoreType.DMA((4,)),
        ),
        flops=1_000_000_000, nbytes=8_000_000,
    )
    rows1 = exchange(pay1)

    half = EP // 2
    full = lambda dims: pl.BlockSpec(dims, lambda i: (0,) * len(dims))
    sel3, rank = call(
        select_cotangent, "select_cotangent", (scal, *cots),
        (shape((EP, CAPZ, D), bf16), shape((8, ZN * TOK), f32)),
        grid=(2,),
        in_specs=[SMEM] + [full((TOK + 8, D))] * 4,
        out_specs=(pl.BlockSpec((half, CAPZ, D), lambda i: (i, 0, 0)), full((8, ZN * TOK))),
        scratch=(pltpu.VMEM((ZN * TOK, D), bf16),),
        flops=1_200_000_000, nbytes=4_000_000,
    )
    got3 = plane_exchange(spread(sel3))
    sel1, gate8 = call(
        select_rows, "select_rows", (scal, rank, *rows1),
        (shape((EP, EXTRA, D), bf16), shape((8, ZN * TOK), f32)),
        grid=(2,),
        in_specs=[SMEM, full((8, ZN * TOK))] + [full((TOK + 16, D))] * 4,
        out_specs=(pl.BlockSpec((half, EXTRA, D), lambda i: (i, 0, 0)), full((8, ZN * TOK))),
        scratch=(pltpu.VMEM((ZN * TOK, D), bf16),),
        flops=1_200_000_000, nbytes=4_000_000,
    )
    got1 = plane_exchange(spread(sel1))

    part = 4
    steps = plane // part
    rows = plane * CAPZ
    spec3 = lambda height: pl.BlockSpec((part, height, D), lambda i: (i, 0, 0))
    spec2 = lambda width: pl.BlockSpec((part * CAPZ, width), lambda i: (i, 0))
    produced, back, act, d_prod, d_gate, d_up = call(
        expert_rows, "expert_rows", (got1, got3, w_gate, w_up, w_down),
        (
            shape((plane, CAPZ, D), bf16), shape((plane, EXTRA, D), bf16),
            shape((rows, hidden_units), bf16), shape((rows, D), bf16),
            shape((rows, hidden_units), bf16), shape((rows, hidden_units), bf16),
        ),
        grid=(steps,),
        in_specs=[
            spec3(EXTRA), spec3(CAPZ), full((D, hidden_units)), full((D, hidden_units)),
            full((hidden_units, D)),
        ],
        out_specs=(
            spec3(CAPZ), spec3(EXTRA), spec2(hidden_units), spec2(D), spec2(hidden_units),
            spec2(hidden_units),
        ),
        flops=12 * rows * D * hidden_units, nbytes=20_000_000,
    )
    sent_back = plane_exchange(back)
    sent_produced = plane_exchange(produced)
    grad_gate, grad_up, grad_down = call(
        expert_weights, "expert_weights", (got1, act, d_prod, d_gate, d_up),
        (
            shape((D, hidden_units), f32), shape((D, hidden_units), f32),
            shape((hidden_units, D), f32),
        ),
        grid=(steps,),
        in_specs=[spec3(EXTRA), spec2(hidden_units), spec2(D), spec2(hidden_units), spec2(hidden_units)],
        out_specs=(full((D, hidden_units)), full((D, hidden_units)), full((hidden_units, D))),
        flops=6 * rows * D * hidden_units, nbytes=14_000_000,
    )
    pay4 = call(
        functools.partial(combine_back, shards), "combine_back", (sent_back, rank),
        shape((ZN, EXTRA, D), bf16),
        grid=(plane // 8,),
        in_specs=[pl.BlockSpec((8, EXTRA, D), lambda i: (i, 0, 0)), full((8, ZN * TOK))],
        out_specs=full((ZN, EXTRA, D)),
        scratch=(pltpu.VMEM((ZN * TOK, D), f32), pltpu.VMEM((8, ZN * TOK), f32)),
        flops=1_200_000_000, nbytes=4_000_000,
    )
    d_parts = [pay4[0]] + [swap(pay4[m], n, m * plane) for m in range(1, ZN)]

    block = D // n
    high = extra_rows(block) + 8
    d_hidden, d_att, grad_o = call(
        hidden_backward, "hidden_backward",
        (scal, *d_parts, hidden1, cotangent, gates, pay1, attended, w_router, gain_m, w_out),
        (shape((TOK, D), f32), shape((TOK, D), bf16), shape((n, high, D), bf16)),
        in_specs=[SMEM] + [VM] * 12,
        flops=600_000_000, nbytes=8_000_000,
    )
    d_tokens, grad_q, grad_kv = call(
        attention_backward, "attention_backward",
        (scal, tokens, gain_a, cosine, sine, q, kd, vd, d_att, d_hidden, w_query, w_key, w_value),
        (shape((TOK, D), bf16), shape((n, block, D), bf16), shape((n, high, D), bf16)),
        in_specs=[SMEM] + [VM] * 9 + [ANY] * 3,
        scratch=(
            pltpu.VMEM((D, D), bf16), pltpu.VMEM((D, D // 2), bf16), pltpu.VMEM((D, D // 2), bf16),
            pltpu.VMEM((TOK, D), bf16), pltpu.VMEM((TOK, D // 2), bf16),
            pltpu.VMEM((TOK, D // 2), bf16), pltpu.SemaphoreType.DMA((3,)),
        ),
        flops=1_500_000_000, nbytes=10_000_000,
    )
    out4 = call(
        functools.partial(combine_output, shards), "combine_output", (sent_produced, rank, gate8),
        shape((ZN, TOK, D), bf16),
        grid=(plane // 8,),
        in_specs=[
            pl.BlockSpec((8, CAPZ, D), lambda i: (i, 0, 0)), full((8, ZN * TOK)),
            full((8, ZN * TOK)),
        ],
        out_specs=full((ZN, TOK, D)),
        scratch=(pltpu.VMEM((ZN * TOK, D), f32),),
        flops=1_200_000_000, nbytes=4_000_000,
    )
    o_parts = [out4[0]] + [swap(out4[m], n, m * plane) for m in range(1, ZN)]
    output = call(
        final_output, "final_output", (hidden1, *o_parts), shape((TOK, D), bf16),
        flops=0, nbytes=2_000_000,
    )

    all_o = gather_back(scatter_sum(grad_o, n, order_o), n, order_o)
    all_q = gather_back(scatter_sum(grad_q, n, order_q), n, order_q)
    all_kv = gather_back(scatter_sum(grad_kv, n, order_kv), n, order_kv)
    g_out, extra_o = call(
        functools.partial(finish_extra, 1, EXPERTS), "finish_out", (scal, all_o),
        (shape((D, D), f32), shape((8 * EXPERTS, D), f32)), in_specs=[SMEM, VM], nbytes=6_000_000,
    )
    g_query = call(
        functools.partial(finish_plain, 2), "finish_query", (scal, all_q),
        shape((D, D), f32), in_specs=[SMEM, VM], nbytes=6_000_000,
    )
    g_key, g_value, extra_kv = call(
        functools.partial(finish_kv, 3), "finish_key_value", (scal, all_kv),
        (shape((D, D // 2), f32), shape((D, D // 2), f32), shape((8, D), f32)),
        in_specs=[SMEM, VM], nbytes=6_000_000,
    )
    extra_o = extra_o.reshape(EXPERTS, 8, D)
    return (
        output, d_tokens, extra_kv[1], g_query, g_key, g_value, g_out, extra_o[0, 1],
        extra_o[:, 0, :].T, grad_gate, grad_up, grad_down,
    )


def solution(mesh):
    in_specs = (
        P("dp", None), P("dp", None), P(), P(), P(), P(), P(), P(), P(),
        P(None, "dp"), P(None, "dp"), P("dp", None), P("dp", None),
    )
    out_specs = (
        P("dp", None), P("dp", None), P(), P(), P(), P(), P(), P(), P(),
        P(None, "dp"), P(None, "dp"), P("dp", None),
    )
    return jax.shard_map(body, mesh=mesh, in_specs=in_specs, out_specs=out_specs, check_vma=False)
```
